256 devices in a mesh: energy: 64 (over z, x, core), atom: 4 (over y).
Axes of the slice: x: 4, y: 4, z: 8, core: 2. Of those that a mesh axis runs over, the one named last changes fastest.
Arguments:
- green_blocks: float32 [256, 32, 34, 288], P('energy', 'atom'), may hold values from -6 to 6
- coupling: float32 [32, 12, 12], P('atom'), may hold values from -1.75 to 1.75
- neighbours: int32 [32, 34], P('atom'), may hold values from 0 to 31
- freq_offset: int32 [64], replicated, may hold values from 1 to 2, as said below
- emit_weight: float32 [64], replicated, may hold values from 0.02 to 0.2
- absorb_weight: float32 [64], replicated, may hold values from 0.02 to 0.2
Outputs:
- sigma: float32 [256, 32, 34, 288], P('energy', 'atom')
The draws below stay inside these ranges and needn't reach their ends.
Inputs may be any that keep to these rules, and one draw needn't show every extreme that they name: `freq_offset`: every offset is 1 or more and at least one offset equals 2.
All inputs are finite; a program needn't handle non-finite values.
Results may differ from the reference program's by a relative error of at most 0.00007.
Values sent between devices are 32-bit elements; how exact they have to be, the bound alone decides.
No kernel may reach another device: no remote copies, remote signals or barrier semaphores. Data moves between devices by JAX's collectives and lax.ppermute only.
A program may use at most 128 MiB of HBM per device.

```python
import math
import jax
import jax.numpy as jnp
from jax import lax

ORB = 12
NBR = 34
NQ = 64
OFF = 2
NE = 256
ATOMS = 32
BLOCK = 288


def draw_freq_offset(key, part):
    values = jax.random.randint(key, (NQ,), 1, OFF + 1).astype(jnp.int32)
    where_top = jax.random.randint(jax.random.fold_in(key, 7), (), 0, NQ)
    return values.at[where_top].set(OFF).astype(jnp.int32)


def place_ends(array, key, low, top_value):
    dims = array.shape
    place = [jax.random.randint(jax.random.fold_in(key, axis), (), 0, dims[axis]) for axis in range(len(dims))]
    array = array.at[tuple(place)].set(low)
    longest = dims.index(max(dims))
    place[longest] = (place[longest] + 1) % dims[longest]
    return array.at[tuple(place)].set(top_value)


def block_scale(rng, shape, split, least, top_value):
    def one(dim, shards_of):
        draws = jax.random.uniform(jax.random.fold_in(jax.random.fold_in(rng, 6), dim), (shards_of,), jnp.float32, least / len(split), top_value / len(split))
        return jnp.repeat(jnp.exp(draws), shape[dim] // shards_of).reshape((-1,) + (1,) * (len(shape) - dim - 1))

    gain = one(*split[0])
    for cut in split[1:]:
        gain = gain * one(*cut)
    return gain


def scatter_about(stream_key, extent, deviation, reach, shards=(), dtype=jnp.bfloat16):
    drawn = jax.random.normal(stream_key, extent, jnp.float32) * deviation
    if len(shards) > 0:
        drawn = block_scale(stream_key, extent, shards, -0.22, 0.18) * drawn
    return jnp.clip(drawn, min=-reach, max=reach).astype(dtype)


def setup_inputs(seed: int = 0) -> dict:
    streams_of = jax.random.split(jax.random.key(seed), 7)
    return {
        "green_blocks": scatter_about(streams_of[0], (NE, ATOMS, NBR, BLOCK), 1.0, 6.0, ((0, 64), (1, 4)), jnp.float32),
        "coupling": scatter_about(streams_of[1], (ATOMS, ORB, ORB), ORB ** -0.5, 1.75, ((0, 4),), jnp.float32),
        "neighbours": place_ends(jax.random.randint(streams_of[2], (ATOMS, NBR), 0, ATOMS), jax.random.fold_in(streams_of[2], 1), 0, ATOMS - 1).astype(jnp.int32),
        "freq_offset": draw_freq_offset(jax.random.fold_in(streams_of[6], 71), 0),
        "emit_weight": jnp.clip(jnp.exp(jax.random.uniform(streams_of[4], (NQ,), jnp.float32, math.log(0.02), math.log(0.2))), 0.02, 0.2),
        "absorb_weight": jnp.clip(jnp.exp(jax.random.uniform(streams_of[5], (NQ,), jnp.float32, math.log(0.02), math.log(0.2))), 0.02, 0.2),
    }


def offset_kernel(freq_offset, emit_weight, absorb_weight):
    shifts = (jnp.arange(2 * OFF + 1) - OFF).astype(jnp.int32)
    emitted = jnp.where(shifts[:, None] == -freq_offset[None, :], emit_weight[None, :], 0.0)
    absorbed = jnp.where(shifts[:, None] == freq_offset[None, :], absorb_weight[None, :], 0.0)
    return jnp.sum(emitted + absorbed, axis=1)


def reference(green_blocks, coupling, neighbours, freq_offset, emit_weight, absorb_weight):
    kernel = offset_kernel(freq_offset, emit_weight, absorb_weight)
    nearby = coupling[neighbours]

    def one_atom(inputs):
        block, left, right = inputs
        parts = block.reshape(NE, NBR, 2, ORB, ORB)
        inner = jnp.einsum("ab,encbd->encad", left, parts, precision=lax.Precision.HIGHEST)
        dressed = jnp.einsum("encad,nfd->encaf", inner, right, precision=lax.Precision.HIGHEST)
        padded = jnp.pad(dressed, ((OFF, OFF), (0, 0), (0, 0), (0, 0), (0, 0)))
        total = jnp.zeros_like(dressed)
        for shift_index in range(2 * OFF + 1):
            total = total + kernel[shift_index] * padded[shift_index:shift_index + NE]
        return total.reshape(NE, NBR, BLOCK)

    result = lax.map(one_atom, (jnp.moveaxis(green_blocks, 1, 0), coupling, nearby))
    return jnp.moveaxis(result, 0, 1)
```

```python
import jax
import jax.numpy as jnp
from jax import lax
from jax.experimental import pallas as pl
from jax.experimental.pallas import tpu as pltpu
from jax.sharding import PartitionSpec as P

OFF = 2
ROWS = 4
ORB = 12
NBR = 34
ATOM = 8
ROW = NBR * ATOM
WIDTH = 288
LANES = 128
TILES = 5
TAIL = 17
PACK = 4 * NBR + TAIL
F32 = jnp.float32
BF16 = jnp.bfloat16


def energy_of(row, core):
    return jnp.where(core == 0, row, ROWS - 1 - row)


def pack_kernel(green, coupling, outer, inner, flat, staged, sem):
    core = lax.axis_index("energy") % 2
    copies = []
    for row in range(2):
        copies.append(pltpu.make_async_copy(green.at[energy_of(row, core)], staged.at[pl.ds(NBR * row, NBR)], sem.at[row]))
    for row in range(2):
        copies.append(pltpu.make_async_copy(green.at[energy_of(3 - row, core)], inner.at[row], sem.at[2 + row]))
    for copy in copies:
        copy.start()
    pieces = [coupling[orbital] for orbital in range(ORB)] + [jnp.zeros((ATOM, 2 * LANES - ORB * ORB), F32)]
    flat[...] = jnp.concatenate(pieces, axis=-1)
    copies[0].wait()
    copies[1].wait()
    outer[0 : 2 * NBR] = staged[:, :, 0:128]
    outer[2 * NBR : 4 * NBR] = staged[:, :, 128:256]
    outer[4 * NBR : PACK] = jnp.concatenate([staged[TAIL * part : TAIL * (part + 1), :, 256:288] for part in range(4)], axis=-1)
    copies[2].wait()
    copies[3].wait()


def dress_tile(tile, natural, result, pair_coef, atom_coef, given, middle, turned):
    rows = pl.ds(pl.multiple_of(tile * LANES, LANES), LANES)
    x_ref, z_ref, y_ref = turned.at[0], middle, turned.at[1]
    x_ref[0:128] = natural[rows, 0:128].T
    x_ref[128:256] = natural[rows, 128:256].T
    x_ref[256:288] = natural[rows, 256:288].T
    low = lax.broadcasted_iota(jnp.int32, (8, LANES), 0) < 4
    x = [[[x_ref[pl.ds(144 * part + 24 * pair + 8 * k, 8)] for k in range(3)] for pair in range(6)] for part in range(2)]
    for a in range(ORB):
        totals = [[None] * 3 for _ in range(2)]
        for pair in range(6):
            first = jnp.broadcast_to(atom_coef[pl.ds(ORB * a + 2 * pair, 1)], (8, LANES))
            last = jnp.broadcast_to(atom_coef[pl.ds(ORB * a + 2 * pair + 1, 1)], (8, LANES))
            coef = (first, jnp.where(low, first, last), last)
            for part in range(2):
                for k in range(3):
                    term = coef[k] * x[part][pair][k]
                    totals[part][k] = term if pair == 0 else totals[part][k] + term
        for part in range(2):
            for k in range(3):
                z_ref[pl.ds((ORB * part + a) * 24 + 8 * k, 8)] = totals[part][k]
    z = []
    for d in range(ORB):
        z.append([z_ref[pl.ds(192 * k + d, 8, stride=24)] + z_ref[pl.ds(192 * k + 12 + d, 8, stride=24)] for k in range(3)])
    for f in range(ORB):
        totals = [None] * 3
        for d in range(ORB):
            coef = jnp.broadcast_to(pair_coef[tile, pl.ds(ORB * f + d, 1)], (8, LANES))
            for k in range(3):
                term = coef * z[d][k]
                totals[k] = term if d == 0 else totals[k] + term
        for k in range(3):
            y_ref[pl.ds(96 * k + f, 8, stride=ORB)] = totals[k]
    if given is not None:
        y_ref[...] = y_ref[...] + given[tile]
    if result is not None:
        result[rows, 0:128] = y_ref[0:128].T
        result[rows, 128:256] = y_ref[128:256].T
        result[rows, 256:288] = y_ref[256:288].T


def kernel_values(freq, emit, absorb, sign):
    sums = []
    for d in range(-OFF, OFF + 1):
        shift = d * sign
        terms = jnp.where(freq == -shift, emit, 0.0) + jnp.where(freq == shift, absorb, 0.0)
        sums.append(jnp.sum(terms, axis=1, keepdims=True))
    return sums


def local_kernel(green, near, flat, from_next, from_second, from_third, neighbours, freq, emit, absorb,
                 out, partial, pair_coef, atom_coef, outer_weights,
                 every, indices, natural, result, middle, turned, sem):
    position = lax.axis_index("energy")
    core = position % 2
    weights = kernel_values(freq[...], emit[...], absorb[...], 1 - 2 * core)
    inside = jnp.where((position > 0) & (position < lax.axis_size("energy") - 1), 1.0, 0.0).astype(F32)
    outer_weights[0] = jnp.broadcast_to(weights[1] * inside, (8, LANES))
    outer_weights[1] = jnp.broadcast_to(weights[0] * inside, (8, LANES))
    every[...] = jnp.zeros_like(every)
    for place, block in enumerate((flat, from_next, from_second, from_third)):
        every[8 * place : 8 * place + 8] = block[...]
    columns = every[...].T[0 : ORB * ORB]
    high = columns.astype(BF16)
    rest = columns - high.astype(F32)
    mid = rest.astype(BF16)
    low = (rest - mid.astype(F32)).astype(BF16)
    indices[...] = jnp.zeros_like(indices)
    indices[:, 0:NBR] = neighbours[...].astype(F32)
    width = TILES * LANES
    lane = lax.broadcasted_iota(jnp.int32, (LANES, width), 1)
    within = lane - jnp.where(lane >= ROW, ROW, 0) - jnp.where(lane >= 2 * ROW, ROW, 0)
    picks = (lax.shift_right_logical(within, 3) == lax.broadcasted_iota(jnp.int32, (LANES, width), 0)).astype(F32).astype(BF16)
    spread = jnp.dot(indices[...].astype(BF16), picks, preferred_element_type=F32)
    lane8 = lax.broadcasted_iota(jnp.int32, (ATOM, width), 1) & 7
    own = lane8 == lax.broadcasted_iota(jnp.int32, (ATOM, width), 0)
    listed = jnp.sum(jnp.where(own, spread, 0.0), axis=0, keepdims=True)
    listed = listed - (lax.axis_index("atom") * ATOM).astype(F32)
    listed = jnp.where(listed < 0, listed + 32.0, listed)
    number = lax.broadcasted_iota(jnp.int32, (LANES, width), 0).astype(F32)
    chosen = (number == listed).astype(F32).astype(BF16)
    spots = (lax.broadcasted_iota(jnp.int32, (LANES, LANES), 0) == (lax.broadcasted_iota(jnp.int32, (LANES, LANES), 1) & 7)).astype(F32).astype(BF16)

    def choose(hot):
        dot = lambda part: jnp.dot(part, hot, preferred_element_type=F32)
        return dot(high) + (dot(mid) + dot(low))

    for tile in range(TILES):
        pair_coef[tile] = choose(chosen[:, LANES * tile : LANES * (tile + 1)])
    atom_coef[...] = choose(spots)

    def rows_of(row):
        return green.at[energy_of(row, core)] if row < ROWS else near.at[row - ROWS]

    def energy_sum(base):
        def step(j, _):
            for half in range(2):
                row = base + half
                total = None
                for d in range(-OFF, OFF + 1):
                    if 0 <= row + d < ROWS + OFF:
                        term = weights[d + OFF] * rows_of(row + d)[j]
                        total = term if total is None else total + term
                natural[pl.ds(pl.multiple_of(ROW * half + 8 * j, 8), 8)] = total
            return 0

        lax.fori_loop(0, NBR, step, 0)

    energy_sum(2)

    def full(tile, _):
        dress_tile(tile, natural, result, pair_coef, atom_coef, None, middle, turned)
        return 0

    lax.fori_loop(0, TILES, full, 0)
    copies = []
    for half in range(2):
        copies.append(pltpu.make_async_copy(result.at[pl.ds(ROW * half, ROW)], out.at[energy_of(2 + half, core)], sem.at[half]))
        copies[-1].start()
    energy_sum(0)

    def part(tile, _):
        dress_tile(tile, natural, None, pair_coef, atom_coef, None, middle, turned)
        partial[tile] = turned[1]
        return 0

    lax.fori_loop(0, TILES, part, 0)
    for copy in copies:
        copy.wait()


def last_kernel(outer, partial, pair_coef, atom_coef, weights, begun, out, natural, result, middle, turned, sem):
    core = lax.axis_index("energy") % 2
    near, far = weights[0], weights[1]
    for half in range(2):
        a = outer[2 * NBR * half : 2 * NBR * half + NBR]
        b = outer[2 * NBR * half + NBR : 2 * NBR * half + 2 * NBR]
        lanes = slice(128 * half, 128 * half + 128)
        natural[0:ROW, lanes] = (near * a + far * b).reshape(ROW, LANES)
        natural[ROW : 2 * ROW, lanes] = (far * a).reshape(ROW, LANES)
    tails = outer[4 * NBR : PACK].reshape(TAIL * 8, LANES)
    near_row, far_row = near[0:1], far[0:1]
    for half in range(2):
        a = tails[:, 32 * half : 32 * half + 32]
        b = tails[:, 64 + 32 * half : 96 + 32 * half]
        natural[TAIL * 8 * half : TAIL * 8 * (half + 1), 256:288] = near_row[:, 0:32] * a + far_row[:, 0:32] * b
        natural[ROW + TAIL * 8 * half : ROW + TAIL * 8 * (half + 1), 256:288] = far_row[:, 0:32] * a

    def full(tile, _):
        dress_tile(tile, natural, result, pair_coef, atom_coef, partial, middle, turned)
        return 0

    copies = [pltpu.make_async_copy(result.at[pl.ds(ROW * half, ROW)], out.at[energy_of(half, core)], sem.at[half]) for half in range(2)]
    lax.fori_loop(0, 3, full, 0)
    copies[0].start()
    lax.fori_loop(3, TILES, full, 0)
    copies[1].start()
    for copy in copies:
        copy.wait()


def local(green_blocks, coupling, neighbours, freq_offset, emit_weight, absorb_weight):
    energies, atoms = lax.axis_size("energy"), lax.axis_size("atom")
    shape = jax.ShapeDtypeStruct
    vmem = pl.BlockSpec(memory_space=pltpu.VMEM)
    anywhere = pl.BlockSpec(memory_space=pl.ANY)
    green = jnp.transpose(green_blocks, (0, 2, 1, 3))
    outer, inner, flat = pl.pallas_call(
        pack_kernel,
        out_shape=(shape((PACK, 8, LANES), F32), shape((2, NBR, ATOM, WIDTH), F32), shape((ATOM, 2 * LANES), F32)),
        in_specs=[anywhere, vmem],
        out_specs=(vmem, vmem, vmem),
        scratch_shapes=[pltpu.VMEM((2 * NBR, ATOM, WIDTH), F32), pltpu.SemaphoreType.DMA((4,))],
        name="pack",
    )(green, jnp.transpose(coupling, (1, 0, 2)))

    pairs = []
    for e in range(energies):
        for a in range(atoms):
            if e in (0, energies - 1):
                to = e * atoms + (a ^ 1)
            else:
                to = (e + 1 if e % 2 else e - 1) * atoms + a
            pairs.append((e * atoms + a, to))
    far = lax.ppermute(outer, ("energy", "atom"), pairs)
    near = lax.ppermute(inner, "energy", [(e, e ^ 1) for e in range(energies)])
    blocks = [lax.ppermute(flat, "atom", [(a, (a - step) % atoms) for a in range(atoms)]) for step in (1, 3, 2)]
    scratch = [pltpu.VMEM((TILES * LANES, WIDTH), F32), pltpu.VMEM((TILES * LANES, WIDTH), F32), pltpu.VMEM((2 * WIDTH, LANES), F32), pltpu.VMEM((2, WIDTH, LANES), F32), pltpu.SemaphoreType.DMA((2,))]
    rows = shape((ROWS, ROW, WIDTH), F32)
    begun, partial, pair_coef, atom_coef, weights = pl.pallas_call(
        local_kernel,
        out_shape=(rows, shape((TILES, WIDTH, LANES), F32), shape((TILES, ORB * ORB, LANES), F32), shape((ORB * ORB, LANES), F32), shape((2, 8, LANES), F32)),
        in_specs=[vmem] * 10,
        out_specs=(anywhere, vmem, vmem, vmem, vmem),
        scratch_shapes=[pltpu.VMEM((LANES, 2 * LANES), F32), pltpu.VMEM((ATOM, LANES), F32)] + scratch,
        name="local",
    )(green, near, flat, blocks[0], blocks[2], blocks[1], neighbours, freq_offset[None], emit_weight[None], absorb_weight[None])
    out = pl.pallas_call(
        last_kernel,
        out_shape=rows,
        in_specs=[vmem] * 5 + [anywhere],
        out_specs=anywhere,
        scratch_shapes=scratch,
        input_output_aliases={5: 0},
        name="last",
    )(far, partial, pair_coef, atom_coef, weights, begun)
    return jnp.transpose(out.reshape(ROWS, NBR, ATOM, WIDTH), (0, 2, 1, 3))


def solution(mesh):
    placed = (
        P("energy", "atom", None, None),
        P("atom", None, None),
        P("atom", None),
        P(),
        P(),
        P(),
    )
    return jax.shard_map(
        local,
        mesh=mesh,
        in_specs=placed,
        out_specs=P("energy", "atom", None, None),
        check_vma=False,
    )
```

```python
import jax
import jax.numpy as jnp
from jax import lax
from jax.experimental import pallas as pl
from jax.experimental.pallas import tpu as pltpu
from jax.sharding import PartitionSpec as P

OFF = 2
ROWS = 4
ORB = 12
NBR = 34
ATOM = 8
ROW = NBR * ATOM
WIDTH = 288
LANES = 128
TILES = 5
TAIL = 17
PACK = 4 * NBR + TAIL
F32 = jnp.float32
BF16 = jnp.bfloat16
GRANT = 16 << 20


def energy_of(row, core):
    return jnp.where(core == 0, row, ROWS - 1 - row)


def pack_kernel(green, outer, fore, rear, sem):
    core = lax.axis_index("energy") % 2
    copies = []
    for row in range(ROWS):
        target = fore.at[row] if row < 2 else rear.at[row - 2]
        copies.append(pltpu.make_async_copy(green.at[energy_of(row, core)], target, sem.at[row]))
    for copy in copies:
        copy.start()
    for row in range(2):
        copies[row].wait()
        outer[NBR * row : NBR * (row + 1)] = fore[row, :, :, 0:128]
        outer[NBR * (2 + row) : NBR * (3 + row)] = fore[row, :, :, 128:256]
    tails = [fore[part // 2, TAIL * (part % 2) : TAIL * (part % 2 + 1), :, 256:288] for part in range(4)]
    outer[4 * NBR : PACK] = jnp.concatenate(tails, axis=-1)
    copies[2].wait()
    copies[3].wait()


def turn_in(tile, natural, x):
    rows = slice(LANES * tile, LANES * (tile + 1))
    x[tile, 0:128] = natural[rows, 0:128].T
    x[tile, 128:256] = natural[rows, 128:256].T
    x[tile, 256:288] = natural[rows, 256:288].T


def turn_out(tile, result, y):
    rows = slice(LANES * tile, LANES * (tile + 1))
    result[rows, 0:128] = y[tile, 0:128].T
    result[rows, 128:256] = y[tile, 128:256].T
    result[rows, 256:288] = y[tile, 256:288].T


def left(tile, atom_coef, x, z):
    low = lax.broadcasted_iota(jnp.int32, (8, LANES), 0) < 4
    for a in range(ORB):
        totals = [[None] * 3 for _ in range(2)]
        for pair in range(6):
            first = jnp.broadcast_to(atom_coef[ORB * a + 2 * pair : ORB * a + 2 * pair + 1], (8, LANES))
            last = jnp.broadcast_to(atom_coef[ORB * a + 2 * pair + 1 : ORB * a + 2 * pair + 2], (8, LANES))
            coef = (first, jnp.where(low, first, last), last)
            for part in range(2):
                for k in range(3):
                    term = coef[k] * x[tile, pl.ds(144 * part + 24 * pair + 8 * k, 8)]
                    totals[part][k] = term if pair == 0 else totals[part][k] + term
        for part in range(2):
            for k in range(3):
                z[tile, pl.ds((ORB * part + a) * 24 + 8 * k, 8)] = totals[part][k]


def right(tile, pair_coef, z, y):
    values = []
    for d in range(ORB):
        values.append([z[tile, pl.ds(192 * k + d, 8, stride=24)] + z[tile, pl.ds(192 * k + 12 + d, 8, stride=24)] for k in range(3)])
    for f in range(ORB):
        totals = [None] * 3
        for d in range(ORB):
            coef = jnp.broadcast_to(pair_coef[tile, ORB * f + d : ORB * f + d + 1], (8, LANES))
            for k in range(3):
                term = coef * values[d][k]
                totals[k] = term if d == 0 else totals[k] + term
        for k in range(3):
            y[tile, pl.ds(96 * k + f, 8, stride=ORB)] = totals[k]


def coupling_rows(block):
    rows = jnp.concatenate([block[orbital] for orbital in range(ORB)] + [jnp.zeros((ATOM, 2 * LANES - ORB * ORB), F32)], axis=-1)
    high = rows.astype(BF16).astype(F32)
    mid = (rows - high).astype(BF16).astype(F32)
    return high, mid, rows - high - mid


def kernel_values(freq, emit, absorb, sign):
    sums = []
    for d in range(-OFF, OFF + 1):
        shift = d * sign
        terms = jnp.where(freq == -shift, emit, 0.0) + jnp.where(freq == shift, absorb, 0.0)
        sums.append(jnp.sum(terms, axis=1, keepdims=True))
    return sums


def sum_kernel(fore, rear, neighbours, freq, emit, absorb, sums, weights, chosen, indices):
    position = lax.axis_index("energy")
    core = position % 2
    weight = kernel_values(freq[...], emit[...], absorb[...], 1 - 2 * core)
    inside = jnp.where((position > 0) & (position < lax.axis_size("energy") - 1), 1.0, 0.0).astype(F32)
    for place, value in enumerate((weight[1] * inside, weight[0] * inside, weight[3], weight[4])):
        weights[place] = jnp.broadcast_to(value, (8, LANES))
    indices[...] = jnp.zeros_like(indices)
    indices[:, 0:NBR] = neighbours[...].astype(F32)
    width = TILES * LANES
    lane = lax.broadcasted_iota(jnp.int32, (LANES, width), 1)
    within = lane - jnp.where(lane >= ROW, ROW, 0) - jnp.where(lane >= 2 * ROW, ROW, 0)
    picks = (lax.shift_right_logical(within, 3) == lax.broadcasted_iota(jnp.int32, (LANES, width), 0)).astype(F32).astype(BF16)
    spread = jnp.dot(indices[...].astype(BF16), picks, preferred_element_type=F32)
    lane8 = lax.broadcasted_iota(jnp.int32, (ATOM, width), 1) & 7
    own = lane8 == lax.broadcasted_iota(jnp.int32, (ATOM, width), 0)
    listed = jnp.sum(jnp.where(own, spread, 0.0), axis=0, keepdims=True)
    listed = listed - (lax.axis_index("atom") * ATOM).astype(F32)
    listed = jnp.where(listed < 0, listed + 32.0, listed)
    number = (lax.broadcasted_iota(jnp.int32, (LANES, width), 0) & 31).astype(F32)
    chosen[:, 0:width] = (number == listed).astype(F32).astype(BF16)
    spots = (lax.broadcasted_iota(jnp.int32, (LANES, LANES), 0) & 31) == (lax.broadcasted_iota(jnp.int32, (LANES, LANES), 1) & 7)
    chosen[:, width : width + LANES] = spots.astype(F32).astype(BF16)

    def step(j, _):
        for sub in range(2):
            values = [fore[0, 2 * j + sub], fore[1, 2 * j + sub], rear[0, 2 * j + sub], rear[1, 2 * j + sub]]
            for row in range(ROWS):
                total = None
                for source in range(ROWS):
                    if abs(source - row) <= OFF:
                        term = weight[source - row + OFF] * values[source]
                        total = term if total is None else total + term
                sums[row, 2 * j + sub] = total
        return 0

    lax.fori_loop(0, NBR // 2, step, 0)


def left_kernel(sums, weights, near, mine, chosen, atom_coef, z, every, natural, x):
    every[...] = jnp.zeros_like(every)
    for place, part in enumerate(coupling_rows(mine)):
        every[32 * place : 32 * place + 8] = part
    columns = every[...].T[0 : ORB * ORB].astype(BF16)
    atom_coef[...] = jnp.dot(columns, chosen[:, LANES * TILES : LANES * (TILES + 1)], preferred_element_type=F32)
    first, second = weights[2][0:1, 0:1], weights[3][0:1, 0:1]

    def step(j, _):
        for sub in range(2):
            place = 2 * j + sub
            a, b = near[1, place], near[0, place]
            natural[pl.ds(pl.multiple_of(8 * place, 8), 8)] = sums[2, place] + second * a
            natural[pl.ds(pl.multiple_of(ROW + 8 * place, 8), 8)] = sums[3, place] + (first * a + second * b)
        return 0

    lax.fori_loop(0, NBR // 2, step, 0)
    turn_in(0, natural, x)
    for tile in range(TILES):
        if tile + 1 < TILES:
            turn_in(tile + 1, natural, x)
        left(tile, atom_coef, x, z)


def sender(result, out, first_row, core, sem):
    copies = [pltpu.make_async_copy(result.at[pl.ds(ROW * half, ROW)], out.at[energy_of(first_row + half, core)], sem.at[half]) for half in range(2)]

    def after(tile):
        if tile == 2:
            copies[0].start()
        if tile == TILES - 1:
            copies[1].start()

    return copies, after


def right_kernel(z, chosen, mine, from_next, from_second, from_third, out, pair_coef, every, result, y, sem):
    position = lax.axis_index("energy")
    crossed = jnp.where((position == 1) | (position == lax.axis_size("energy") - 2), 1, 0)
    for place, block in ((0, mine), (1 + 2 * crossed, from_next), (2, from_second), (3 - 2 * crossed, from_third)):
        for part, rows in enumerate(coupling_rows(block)):
            every[pl.ds(pl.multiple_of(32 * part + 8 * place, 8), 8)] = rows
    every[96:128] = jnp.zeros((32, 2 * LANES), F32)
    columns = every[...].T[0 : ORB * ORB].astype(BF16)
    for tile in range(TILES):
        pair_coef[tile] = jnp.dot(columns, chosen[:, LANES * tile : LANES * (tile + 1)], preferred_element_type=F32)
    copies, after = sender(result, out, 2, lax.axis_index("energy") % 2, sem)
    for tile in range(TILES):
        right(tile, pair_coef, z, y)
        turn_out(tile, result, y)
        after(tile)
    for copy in copies:
        copy.wait()


def last_kernel(outer, sums, pair_coef, atom_coef, weights, begun, out, natural, result, x, z, y, sem):
    near, far = weights[0], weights[1]
    for half in range(2):
        a = outer[2 * NBR * half : 2 * NBR * half + NBR]
        b = outer[2 * NBR * half + NBR : 2 * NBR * half + 2 * NBR]
        lanes = slice(128 * half, 128 * half + 128)
        natural[0:ROW, lanes] = (sums[0, :, :, lanes] + (near * a + far * b)).reshape(ROW, LANES)
        natural[ROW : 2 * ROW, lanes] = (sums[1, :, :, lanes] + far * a).reshape(ROW, LANES)
    near_part, far_part = near[0:1, 0:32], far[0:1, 0:32]
    for half in range(2):
        a = outer[4 * NBR : PACK, :, 32 * half : 32 * half + 32]
        b = outer[4 * NBR : PACK, :, 64 + 32 * half : 96 + 32 * half]
        rows = slice(TAIL * 8 * half, TAIL * 8 * (half + 1))
        tiles = slice(TAIL * half, TAIL * (half + 1))
        natural[rows, 256:288] = (sums[0, tiles, :, 256:288] + (near_part * a + far_part * b)).reshape(TAIL * 8, 32)
        rows = slice(ROW + TAIL * 8 * half, ROW + TAIL * 8 * (half + 1))
        natural[rows, 256:288] = (sums[1, tiles, :, 256:288] + far_part * a).reshape(TAIL * 8, 32)
    copies, after = sender(result, out, 0, lax.axis_index("energy") % 2, sem)
    turn_in(0, natural, x)
    for tile in range(TILES):
        if tile + 1 < TILES:
            turn_in(tile + 1, natural, x)
        left(tile, atom_coef, x, z)
        right(tile, pair_coef, z, y)
        turn_out(tile, result, y)
        after(tile)
    for copy in copies:
        copy.wait()


def held(value):
    return pltpu.with_memory_space_constraint(value, pltpu.VMEM)


def planned(green_blocks, coupling, neighbours, freq_offset, emit_weight, absorb_weight):
    energies, atoms = lax.axis_size("energy"), lax.axis_size("atom")
    shape = lambda dims, dtype=F32: pltpu.VMEM(dims, dtype)
    vmem = pl.BlockSpec(memory_space=pltpu.VMEM)
    anywhere = pl.BlockSpec(memory_space=pl.ANY)
    green = jnp.transpose(green_blocks, (0, 2, 1, 3))
    mine = jnp.transpose(coupling, (1, 0, 2))
    ends = {0: 1, energies - 1: energies - 2}
    others = {other: end for end, other in ends.items()}
    up, down = [], []
    for e in range(energies):
        for a in range(atoms):
            here, above, below = e * atoms + a, (a + 1) % atoms, (a - 1) % atoms
            if e in ends:
                up.append((here, ends[e] * atoms + below))
                down.append((here, e * atoms + below))
            elif e in others:
                up.append((here, others[e] * atoms + above))
                down.append((here, e * atoms + above))
            else:
                up.append((here, e * atoms + above))
                down.append((here, e * atoms + below))
    third = lax.ppermute(mine, ("energy", "atom"), up)
    first = lax.ppermute(mine, ("energy", "atom"), down)
    outer, fore, rear = pl.pallas_call(
        pack_kernel,
        out_shape=(shape((PACK, 8, LANES)), shape((2, NBR, ATOM, WIDTH)), shape((2, NBR, ATOM, WIDTH))),
        in_specs=[pl.BlockSpec(memory_space=pltpu.HBM)],
        out_specs=(vmem, vmem, vmem),
        scratch_shapes=[pltpu.SemaphoreType.DMA((ROWS,))],
        compiler_params=pltpu.CompilerParams(vmem_limit_bytes=GRANT),
        name="pack",
    )(pltpu.with_memory_space_constraint(green, pltpu.HBM))

    pairs = []
    for e in range(energies):
        for a in range(atoms):
            if e in (0, energies - 1):
                to = e * atoms + (a + 1) % atoms
            else:
                to = (e + 1 if e % 2 else e - 1) * atoms + a
            pairs.append((e * atoms + a, to))
    far = lax.ppermute(outer, ("energy", "atom"), pairs)
    near = lax.ppermute(rear, "energy", [(e, e ^ 1) for e in range(energies)])
    second = lax.ppermute(mine, "atom", [(a, (a + 2) % atoms) for a in range(atoms)])
    sums, weights, chosen = pl.pallas_call(
        sum_kernel,
        out_shape=(shape((ROWS, NBR, ATOM, WIDTH)), shape((4, 8, LANES)), shape((LANES, (TILES + 1) * LANES), BF16)),
        in_specs=[vmem] * 6,
        out_specs=(vmem, vmem, vmem),
        scratch_shapes=[pltpu.VMEM((ATOM, LANES), F32)],
        compiler_params=pltpu.CompilerParams(vmem_limit_bytes=GRANT),
        name="sums",
    )(fore, rear, neighbours, freq_offset[None], emit_weight[None], absorb_weight[None])
    turned = pltpu.VMEM((TILES, WIDTH, LANES), F32)
    halfway = shape((TILES, 2 * WIDTH, LANES))
    rowwise = pltpu.VMEM((TILES * LANES, WIDTH), F32)
    table = pltpu.VMEM((LANES, 2 * LANES), F32)
    rows = jax.ShapeDtypeStruct((ROWS, ROW, WIDTH), F32)
    atom_coef, z = pl.pallas_call(
        left_kernel,
        out_shape=(shape((ORB * ORB, LANES)), halfway),
        in_specs=[vmem] * 5,
        out_specs=(vmem, vmem),
        scratch_shapes=[table, rowwise, turned],
        compiler_params=pltpu.CompilerParams(vmem_limit_bytes=GRANT),
        name="left",
    )(*map(held, (sums, weights, near, mine, chosen)))
    begun, pair_coef = pl.pallas_call(
        right_kernel,
        out_shape=(rows, shape((TILES, ORB * ORB, LANES))),
        in_specs=[vmem] * 6,
        out_specs=(anywhere, vmem),
        scratch_shapes=[table, rowwise, turned, pltpu.SemaphoreType.DMA((2,))],
        compiler_params=pltpu.CompilerParams(vmem_limit_bytes=GRANT),
        name="right",
    )(*map(held, (z, chosen, mine, first, second, third)))
    out = pl.pallas_call(
        last_kernel,
        out_shape=rows,
        in_specs=[vmem] * 5 + [anywhere],
        out_specs=anywhere,
        scratch_shapes=[rowwise, rowwise, turned, halfway, turned, pltpu.SemaphoreType.DMA((2,))],
        input_output_aliases={5: 0},
        compiler_params=pltpu.CompilerParams(vmem_limit_bytes=GRANT),
        name="last",
    )(*map(held, (far, sums, pair_coef, atom_coef, weights)), begun)
    return jnp.transpose(out.reshape(ROWS, NBR, ATOM, WIDTH), (0, 2, 1, 3))


def solution(mesh):
    placed = (
        P("energy", "atom", None, None),
        P("atom", None, None),
        P("atom", None),
        P(),
        P(),
        P(),
    )
    return jax.shard_map(
        planned,
        mesh=mesh,
        in_specs=placed,
        out_specs=P("energy", "atom", None, None),
        check_vma=False,
    )
```

```python
import jax
import jax.numpy as jnp
from jax import lax
from jax.experimental import pallas as pl
from jax.experimental.pallas import tpu as pltpu
from jax.sharding import PartitionSpec as P

OFF = 2
ROWS = 4
ORB = 12
NBR = 34
ATOM = 8
ROW = NBR * ATOM
WIDTH = 288
LANES = 128
TILES = 5
TAIL = 17
PACK = 4 * NBR + TAIL
F32 = jnp.float32
BF16 = jnp.bfloat16
GRANT = 16 << 20


def energy_of(row, core):
    return jnp.where(core == 0, row, ROWS - 1 - row)


def pack_kernel(green, coupling, outer, fore, rear, flat, matrices, sem):
    core = lax.axis_index("energy") % 2
    copies = []
    for row in range(ROWS):
        target = fore.at[row] if row < 2 else rear.at[row - 2]
        copies.append(pltpu.make_async_copy(green.at[energy_of(row, core)], target, sem.at[row]))
    copies.append(pltpu.make_async_copy(coupling, matrices, sem.at[ROWS]))
    for place in (4, 0, 1, 2, 3):
        copies[place].start()
    copies[4].wait()
    pieces = [matrices[orbital] for orbital in range(ORB)] + [jnp.zeros((ATOM, 2 * LANES - ORB * ORB), F32)]
    flat[...] = jnp.concatenate(pieces, axis=-1)
    for row in range(2):
        copies[row].wait()
        outer[NBR * row : NBR * (row + 1)] = fore[row, :, :, 0:128]
        outer[NBR * (2 + row) : NBR * (3 + row)] = fore[row, :, :, 128:256]
    tails = [fore[part // 2, TAIL * (part % 2) : TAIL * (part % 2 + 1), :, 256:288] for part in range(4)]
    outer[4 * NBR : PACK] = jnp.concatenate(tails, axis=-1)
    copies[2].wait()
    copies[3].wait()


def turn_in(tile, natural, x):
    rows = slice(LANES * tile, LANES * (tile + 1))
    x[tile, 0:128] = natural[rows, 0:128].T
    x[tile, 128:256] = natural[rows, 128:256].T
    x[tile, 256:288] = natural[rows, 256:288].T


def turn_out(tile, result, y):
    rows = slice(LANES * tile, LANES * (tile + 1))
    result[rows, 0:128] = y[tile, 0:128].T
    result[rows, 128:256] = y[tile, 128:256].T
    result[rows, 256:288] = y[tile, 256:288].T


def left(tile, atom_coef, x, z):
    low = lax.broadcasted_iota(jnp.int32, (8, LANES), 0) < 4
    for a in range(ORB):
        totals = [[None] * 3 for _ in range(2)]
        for pair in range(6):
            first = jnp.broadcast_to(atom_coef[ORB * a + 2 * pair : ORB * a + 2 * pair + 1], (8, LANES))
            last = jnp.broadcast_to(atom_coef[ORB * a + 2 * pair + 1 : ORB * a + 2 * pair + 2], (8, LANES))
            coef = (first, jnp.where(low, first, last), last)
            for part in range(2):
                for k in range(3):
                    term = coef[k] * x[tile, pl.ds(144 * part + 24 * pair + 8 * k, 8)]
                    totals[part][k] = term if pair == 0 else totals[part][k] + term
        for part in range(2):
            for k in range(3):
                z[tile, pl.ds((ORB * part + a) * 24 + 8 * k, 8)] = totals[part][k]


def right(tile, pair_coef, z, y):
    values = []
    for d in range(ORB):
        values.append([z[tile, pl.ds(192 * k + d, 8, stride=24)] + z[tile, pl.ds(192 * k + 12 + d, 8, stride=24)] for k in range(3)])
    for f in range(ORB):
        totals = [None] * 3
        for d in range(ORB):
            coef = jnp.broadcast_to(pair_coef[tile, ORB * f + d : ORB * f + d + 1], (8, LANES))
            for k in range(3):
                term = coef * values[d][k]
                totals[k] = term if d == 0 else totals[k] + term
        for k in range(3):
            y[tile, pl.ds(96 * k + f, 8, stride=ORB)] = totals[k]


def three_parts(rows):
    high = rows.astype(BF16).astype(F32)
    mid = (rows - high).astype(BF16).astype(F32)
    return high, mid, rows - high - mid


def kernel_values(freq, emit, absorb, sign):
    sums = []
    for d in range(-OFF, OFF + 1):
        shift = d * sign
        terms = jnp.where(freq == -shift, emit, 0.0) + jnp.where(freq == shift, absorb, 0.0)
        sums.append(jnp.sum(terms, axis=1, keepdims=True))
    return sums


def left_kernel(fore, rear, near, neighbours, freq, emit, absorb, mine, sums, weights, chosen, atom_coef, z,
                indices, every, natural, x):
    position = lax.axis_index("energy")
    core = position % 2
    weight = kernel_values(freq[...], emit[...], absorb[...], 1 - 2 * core)
    inside = jnp.where((position > 0) & (position < lax.axis_size("energy") - 1), 1.0, 0.0).astype(F32)
    for place, value in enumerate((weight[1] * inside, weight[0] * inside)):
        weights[place] = jnp.broadcast_to(value, (8, LANES))
    indices[...] = jnp.zeros_like(indices)
    indices[:, 0:NBR] = neighbours[...].astype(F32)
    width = TILES * LANES
    lane = lax.broadcasted_iota(jnp.int32, (LANES, width), 1)
    within = lane - jnp.where(lane >= ROW, ROW, 0) - jnp.where(lane >= 2 * ROW, ROW, 0)
    picks = (lax.shift_right_logical(within, 3) == lax.broadcasted_iota(jnp.int32, (LANES, width), 0)).astype(F32).astype(BF16)
    spread = jnp.dot(indices[...].astype(BF16), picks, preferred_element_type=F32)
    lane8 = lax.broadcasted_iota(jnp.int32, (ATOM, width), 1) & 7
    own = lane8 == lax.broadcasted_iota(jnp.int32, (ATOM, width), 0)
    listed = jnp.sum(jnp.where(own, spread, 0.0), axis=0, keepdims=True)
    listed = listed - (lax.axis_index("atom") * ATOM).astype(F32)
    listed = jnp.where(listed < 0, listed + 32.0, listed)
    number = (lax.broadcasted_iota(jnp.int32, (LANES, width), 0) & 31).astype(F32)
    chosen[:, 0:width] = (number == listed).astype(F32).astype(BF16)
    spots = (lax.broadcasted_iota(jnp.int32, (LANES, LANES), 0) & 31) == (lax.broadcasted_iota(jnp.int32, (LANES, LANES), 1) & 7)
    chosen[:, width : width + LANES] = spots.astype(F32).astype(BF16)

    every[...] = jnp.zeros_like(every)
    for place, part in enumerate(three_parts(mine[...])):
        every[32 * place : 32 * place + 8] = part
    columns = every[...].T[0 : ORB * ORB].astype(BF16)
    atom_coef[...] = jnp.dot(columns, chosen[:, width : width + LANES], preferred_element_type=F32)
    for j in range(NBR):
        values = [fore[0, j], fore[1, j], rear[0, j], rear[1, j], near[1, j], near[0, j]]
        for row in range(ROWS):
            total = None
            for source in range(ROWS + OFF):
                if abs(source - row) <= OFF:
                    term = weight[source - row + OFF] * values[source]
                    total = term if total is None else total + term
            if row < 2:
                sums[row, j] = total
            else:
                natural[ROW * (row - 2) + 8 * j : ROW * (row - 2) + 8 * j + 8] = total
    turn_in(0, natural, x)
    for tile in range(TILES):
        if tile + 1 < TILES:
            turn_in(tile + 1, natural, x)
        left(tile, atom_coef, x, z)


def sender(result, out, first_row, core, sem):
    pieces = []
    for tile in range(TILES):
        for half in range(2):
            low, high = max(LANES * tile, ROW * half), min(LANES * (tile + 1), ROW * (half + 1))
            if low < high:
                target = out.at[energy_of(first_row + half, core), pl.ds(low - ROW * half, high - low)]
                pieces.append((tile, pltpu.make_async_copy(result.at[pl.ds(low, high - low)], target, sem.at[len(pieces)])))

    def after(tile):
        for ready, piece in pieces:
            if ready == tile:
                piece.start()

    return [piece for _, piece in pieces], after


def right_kernel(z, chosen, mine, from_next, from_second, from_third, out, pair_coef, every, result, y, sem):
    position = lax.axis_index("energy")
    crossed = jnp.where((position == 1) | (position == lax.axis_size("energy") - 2), 1, 0)
    for place, block in ((0, mine), (1 + 2 * crossed, from_next), (2, from_second), (3 - 2 * crossed, from_third)):
        for part, rows in enumerate(three_parts(block[...])):
            every[pl.ds(pl.multiple_of(32 * part + 8 * place, 8), 8)] = rows
    every[96:128] = jnp.zeros((32, 2 * LANES), F32)
    columns = every[...].T[0 : ORB * ORB].astype(BF16)
    for tile in range(TILES):
        pair_coef[tile] = jnp.dot(columns, chosen[:, LANES * tile : LANES * (tile + 1)], preferred_element_type=F32)
    copies, after = sender(result, out, 2, lax.axis_index("energy") % 2, sem)
    for tile in range(TILES):
        right(tile, pair_coef, z, y)
        turn_out(tile, result, y)
        after(tile)
    for copy in copies:
        copy.wait()


def last_kernel(outer, sums, pair_coef, atom_coef, weights, begun, out, natural, result, x, z, y, sem):
    near, far = weights[0], weights[1]
    for half in range(2):
        a = outer[2 * NBR * half : 2 * NBR * half + NBR]
        b = outer[2 * NBR * half + NBR : 2 * NBR * half + 2 * NBR]
        lanes = slice(128 * half, 128 * half + 128)
        natural[0:ROW, lanes] = (sums[0, :, :, lanes] + (near * a + far * b)).reshape(ROW, LANES)
        natural[ROW : 2 * ROW, lanes] = (sums[1, :, :, lanes] + far * a).reshape(ROW, LANES)
    near_part, far_part = near[0:1, 0:32], far[0:1, 0:32]
    for half in range(2):
        a = outer[4 * NBR : PACK, :, 32 * half : 32 * half + 32]
        b = outer[4 * NBR : PACK, :, 64 + 32 * half : 96 + 32 * half]
        rows = slice(TAIL * 8 * half, TAIL * 8 * (half + 1))
        tiles = slice(TAIL * half, TAIL * (half + 1))
        natural[rows, 256:288] = (sums[0, tiles, :, 256:288] + (near_part * a + far_part * b)).reshape(TAIL * 8, 32)
        rows = slice(ROW + TAIL * 8 * half, ROW + TAIL * 8 * (half + 1))
        natural[rows, 256:288] = (sums[1, tiles, :, 256:288] + far_part * a).reshape(TAIL * 8, 32)
    copies, after = sender(result, out, 0, lax.axis_index("energy") % 2, sem)
    turn_in(0, natural, x)
    for tile in range(TILES):
        if tile + 1 < TILES:
            turn_in(tile + 1, natural, x)
        left(tile, atom_coef, x, z)
        right(tile, pair_coef, z, y)
        turn_out(tile, result, y)
        after(tile)
    for copy in copies:
        copy.wait()


def held(value):
    return pltpu.with_memory_space_constraint(value, pltpu.VMEM)


def planned(green_blocks, coupling, neighbours, freq_offset, emit_weight, absorb_weight):
    energies, atoms = lax.axis_size("energy"), lax.axis_size("atom")
    shape = lambda dims, dtype=F32: pltpu.VMEM(dims, dtype)
    vmem = pl.BlockSpec(memory_space=pltpu.VMEM)
    anywhere = pl.BlockSpec(memory_space=pl.ANY)
    green = jnp.transpose(green_blocks, (0, 2, 1, 3))
    outer, fore, rear, mine = pl.pallas_call(
        pack_kernel,
        out_shape=(shape((PACK, 8, LANES)), shape((2, NBR, ATOM, WIDTH)), shape((2, NBR, ATOM, WIDTH)), shape((ATOM, 2 * LANES))),
        in_specs=[anywhere] * 2,
        out_specs=(vmem,) * 4,
        scratch_shapes=[pltpu.VMEM((ORB, ATOM, ORB), F32), pltpu.SemaphoreType.DMA((ROWS + 1,))],
        compiler_params=pltpu.CompilerParams(vmem_limit_bytes=GRANT),
        name="pack",
    )(*(pltpu.with_memory_space_constraint(array, pltpu.HBM) for array in (green, jnp.transpose(coupling, (1, 0, 2)))))

    ends = {0: 1, energies - 1: energies - 2}
    others = {other: end for end, other in ends.items()}
    up, down = [], []
    for e in range(energies):
        for a in range(atoms):
            here, above, below = e * atoms + a, (a + 1) % atoms, (a - 1) % atoms
            if e in ends and a % 2:
                up.append((here, ends[e] * atoms + below))
                down.append((here, e * atoms + below))
            elif e in ends:
                up.append((here, e * atoms + above))
                down.append((here, ends[e] * atoms + above))
            elif e in others and a % 2:
                up.append((here, others[e] * atoms + above))
                down.append((here, e * atoms + above))
            elif e in others:
                up.append((here, e * atoms + below))
                down.append((here, others[e] * atoms + below))
            else:
                up.append((here, e * atoms + above))
                down.append((here, e * atoms + below))
    third = lax.ppermute(mine, ("energy", "atom"), up)
    first = lax.ppermute(mine, ("energy", "atom"), down)
    pairs = []
    for e in range(energies):
        for a in range(atoms):
            if e in (0, energies - 1):
                to = e * atoms + atoms - 1 - a
            else:
                to = (e + 1 if e % 2 else e - 1) * atoms + a
            pairs.append((e * atoms + a, to))
    far = lax.ppermute(outer, ("energy", "atom"), pairs)
    near = lax.ppermute(rear, "energy", [(e, e ^ 1) for e in range(energies)])
    second = lax.ppermute(mine, "atom", [(a, (a + 2) % atoms) for a in range(atoms)])
    turned = pltpu.VMEM((TILES, WIDTH, LANES), F32)
    halfway = shape((TILES, 2 * WIDTH, LANES))
    rowwise = pltpu.VMEM((TILES * LANES, WIDTH), F32)
    table = pltpu.VMEM((LANES, 2 * LANES), F32)
    rows = jax.ShapeDtypeStruct((ROWS, ROW, WIDTH), F32)
    sums, weights, chosen, atom_coef, z = pl.pallas_call(
        left_kernel,
        out_shape=(shape((2, NBR, ATOM, WIDTH)), shape((2, 8, LANES)), shape((LANES, (TILES + 1) * LANES), BF16), shape((ORB * ORB, LANES)), halfway),
        in_specs=[vmem] * 8,
        out_specs=(vmem,) * 5,
        scratch_shapes=[pltpu.VMEM((ATOM, LANES), F32), table, rowwise, turned],
        compiler_params=pltpu.CompilerParams(vmem_limit_bytes=GRANT),
        name="left",
    )(*map(held, (fore, rear, near)), neighbours, freq_offset[None], emit_weight[None], absorb_weight[None], held(mine))
    begun, pair_coef = pl.pallas_call(
        right_kernel,
        out_shape=(rows, shape((TILES, ORB * ORB, LANES))),
        in_specs=[vmem] * 6,
        out_specs=(anywhere, vmem),
        scratch_shapes=[table, rowwise, turned, pltpu.SemaphoreType.DMA((TILES + 1,))],
        compiler_params=pltpu.CompilerParams(vmem_limit_bytes=GRANT),
        name="right",
    )(*map(held, (z, chosen, mine, first, second, third)))
    out = pl.pallas_call(
        last_kernel,
        out_shape=rows,
        in_specs=[vmem] * 5 + [anywhere],
        out_specs=anywhere,
        scratch_shapes=[rowwise, rowwise, turned, halfway, turned, pltpu.SemaphoreType.DMA((TILES + 1,))],
        input_output_aliases={5: 0},
        compiler_params=pltpu.CompilerParams(vmem_limit_bytes=GRANT),
        name="last",
    )(*map(held, (far, sums, pair_coef, atom_coef, weights)), begun)
    return jnp.transpose(out.reshape(ROWS, NBR, ATOM, WIDTH), (0, 2, 1, 3))


def solution(mesh):
    placed = (
        P("energy", "atom", None, None),
        P("atom", None, None),
        P("atom", None),
        P(),
        P(),
        P(),
    )
    return jax.shard_map(
        planned,
        mesh=mesh,
        in_specs=placed,
        out_specs=P("energy", "atom", None, None),
        check_vma=False,
    )
```

```python
import jax
import jax.numpy as jnp
from jax import lax
from jax.experimental import pallas as pl
from jax.experimental.pallas import tpu as pltpu
from jax.sharding import PartitionSpec as P

OFF = 2
ROWS = 4
ORB = 12
NBR = 34
ATOM = 8
ROW = NBR * ATOM
WIDTH = 288
LANES = 128
TILES = 5
TAIL = 17
PACK = 4 * NBR + TAIL
F32 = jnp.float32
BF16 = jnp.bfloat16
GRANT = 16 << 20


def energy_of(row, core):
    return jnp.where(core == 0, row, ROWS - 1 - row)


def pack_kernel(green, coupling, outer, fore, rear, flat, matrices, sem):
    core = lax.axis_index("energy") % 2
    copies = []
    for row in range(ROWS):
        target = fore.at[row] if row < 2 else rear.at[row - 2]
        copies.append(pltpu.make_async_copy(green.at[energy_of(row, core)], target, sem.at[row]))
    copies.append(pltpu.make_async_copy(coupling, matrices, sem.at[ROWS]))
    for place in (4, 0, 1, 2, 3):
        copies[place].start()
    copies[4].wait()
    pieces = [matrices[orbital] for orbital in range(ORB)] + [jnp.zeros((ATOM, 2 * LANES - ORB * ORB), F32)]
    flat[...] = jnp.concatenate(pieces, axis=-1)
    for row in range(2):
        copies[row].wait()
        outer[NBR * row : NBR * (row + 1)] = fore[row, :, :, 0:128]
        outer[NBR * (2 + row) : NBR * (3 + row)] = fore[row, :, :, 128:256]
    tails = [fore[part // 2, TAIL * (part % 2) : TAIL * (part % 2 + 1), :, 256:288] for part in range(4)]
    outer[4 * NBR : PACK] = jnp.concatenate(tails, axis=-1)
    copies[2].wait()
    copies[3].wait()


def filled(tile):
    return min(LANES, 2 * ROW - LANES * tile)


def turn_in(tile, natural, x):
    size = filled(tile)
    rows = slice(LANES * tile, LANES * tile + size)
    x[tile, 0:128, 0:size] = natural[rows, 0:128].T
    x[tile, 128:256, 0:size] = natural[rows, 128:256].T
    x[tile, 256:288, 0:size] = natural[rows, 256:288].T


def turn_out(tile, result, y):
    size = filled(tile)
    rows = slice(LANES * tile, LANES * tile + size)
    result[rows, 0:128] = y[tile, 0:128, 0:size].T
    result[rows, 128:256] = y[tile, 128:256, 0:size].T
    result[rows, 256:288] = y[tile, 256:288, 0:size].T


def blocks_of(tile):
    return [divmod(block, NBR) for block in range(16 * tile, 16 * tile + filled(tile) // 8)]


def left(tile, atom_coef, x, z):
    low = lax.broadcasted_iota(jnp.int32, (8, LANES), 0) < 4
    for block in range(0, ORB, 6):
        totals = {}
        for pair in range(6):
            values = [[x[tile, pl.ds(144 * part + 24 * pair + 8 * k, 8)] for k in range(3)] for part in range(2)]
            for a in range(block, block + 6):
                first = jnp.broadcast_to(atom_coef[ORB * a + 2 * pair : ORB * a + 2 * pair + 1], (8, LANES))
                last = jnp.broadcast_to(atom_coef[ORB * a + 2 * pair + 1 : ORB * a + 2 * pair + 2], (8, LANES))
                coef = (first, jnp.where(low, first, last), last)
                for part in range(2):
                    for k in range(3):
                        term = coef[k] * values[part][k]
                        totals[a, part, k] = term if pair == 0 else totals[a, part, k] + term
        for (a, part, k), total in totals.items():
            z[tile, pl.ds((ORB * part + a) * 24 + 8 * k, 8)] = total


def right(tile, pair_coef, z, y):
    totals = {}
    for d in range(ORB):
        values = [z[tile, pl.ds(192 * k + d, 8, stride=24)] + z[tile, pl.ds(192 * k + 12 + d, 8, stride=24)] for k in range(3)]
        for f in range(ORB):
            coef = jnp.broadcast_to(pair_coef[tile, ORB * f + d : ORB * f + d + 1], (8, LANES))
            for k in range(3):
                term = coef * values[k]
                totals[f, k] = term if d == 0 else totals[f, k] + term
    for (f, k), total in totals.items():
        y[tile, pl.ds(96 * k + f, 8, stride=ORB)] = total


def three_parts(rows):
    high = rows.astype(BF16).astype(F32)
    mid = (rows - high).astype(BF16).astype(F32)
    return high, mid, rows - high - mid


def kernel_values(freq, emit, absorb, sign):
    sums = []
    for d in range(-OFF, OFF + 1):
        shift = d * sign
        terms = jnp.where(freq == -shift, emit, 0.0) + jnp.where(freq == shift, absorb, 0.0)
        sums.append(jnp.sum(terms, axis=1, keepdims=True))
    return sums


def left_kernel(fore, rear, near, neighbours, freq, emit, absorb, mine, sums, weights, chosen, atom_coef, z,
                indices, every, natural, x):
    position = lax.axis_index("energy")
    core = position % 2
    weight = kernel_values(freq[...], emit[...], absorb[...], 1 - 2 * core)
    inside = jnp.where((position > 0) & (position < lax.axis_size("energy") - 1), 1.0, 0.0).astype(F32)
    for place, value in enumerate((weight[1] * inside, weight[0] * inside)):
        weights[place] = jnp.broadcast_to(value, (8, LANES))
    indices[...] = jnp.zeros_like(indices)
    indices[:, 0:NBR] = neighbours[...].astype(F32)
    width = TILES * LANES
    lane = lax.broadcasted_iota(jnp.int32, (LANES, width), 1)
    within = lane - jnp.where(lane >= ROW, ROW, 0) - jnp.where(lane >= 2 * ROW, ROW, 0)
    picks = (lax.shift_right_logical(within, 3) == lax.broadcasted_iota(jnp.int32, (LANES, width), 0)).astype(F32).astype(BF16)
    spread = jnp.dot(indices[...].astype(BF16), picks, preferred_element_type=F32)
    lane8 = lax.broadcasted_iota(jnp.int32, (ATOM, width), 1) & 7
    own = lane8 == lax.broadcasted_iota(jnp.int32, (ATOM, width), 0)
    listed = jnp.sum(jnp.where(own, spread, 0.0), axis=0, keepdims=True)
    listed = listed - (lax.axis_index("atom") * ATOM).astype(F32)
    listed = jnp.where(listed < 0, listed + 32.0, listed)
    number = (lax.broadcasted_iota(jnp.int32, (LANES, width), 0) & 31).astype(F32)
    chosen[:, 0:width] = (number == listed).astype(F32).astype(BF16)
    spots = (lax.broadcasted_iota(jnp.int32, (LANES, LANES), 0) & 31) == (lax.broadcasted_iota(jnp.int32, (LANES, LANES), 1) & 7)
    chosen[:, width : width + LANES] = spots.astype(F32).astype(BF16)

    every[...] = jnp.zeros_like(every)
    for place, part in enumerate(three_parts(mine[...])):
        every[32 * place : 32 * place + 8] = part
    columns = every[...].T[0 : ORB * ORB].astype(BF16)
    atom_coef[...] = jnp.dot(columns, chosen[:, width : width + LANES], preferred_element_type=F32)
    sources = [(fore, 0), (fore, 1), (rear, 0), (rear, 1), (near, 1), (near, 0)]

    def energy_sum(row, j):
        total = None
        for source in range(max(0, row - OFF), min(ROWS + OFF, row + OFF + 1)):
            ref, place = sources[source]
            term = weight[source - row + OFF] * ref[place, j]
            total = term if total is None else total + term
        return total

    def prepare(tile):
        for row, j in blocks_of(tile):
            natural[ROW * row + 8 * j : ROW * row + 8 * j + 8] = energy_sum(2 + row, j)
            sums[row, j] = energy_sum(row, j)
        turn_in(tile, natural, x)

    prepare(0)
    for tile in range(TILES):
        if tile + 1 < TILES:
            prepare(tile + 1)
        left(tile, atom_coef, x, z)


def sender(result, out, first_row, core, sem):
    pieces = []
    for tile in range(TILES):
        for half in range(2):
            low, high = max(LANES * tile, ROW * half), min(LANES * (tile + 1), ROW * (half + 1))
            if low < high:
                target = out.at[energy_of(first_row + half, core), pl.ds(low - ROW * half, high - low)]
                pieces.append((tile, pltpu.make_async_copy(result.at[pl.ds(low, high - low)], target, sem.at[len(pieces)])))

    def after(tile):
        for ready, piece in pieces:
            if ready == tile:
                piece.start()

    return [piece for _, piece in pieces], after


def right_kernel(z, chosen, mine, from_next, from_second, from_third, result, pair_coef, every, y):
    position = lax.axis_index("energy")
    crossed = jnp.where((position == 1) | (position == lax.axis_size("energy") - 2), 1, 0)
    for place, block in ((0, mine), (1 + 2 * crossed, from_next), (2, from_second), (3 - 2 * crossed, from_third)):
        for part, rows in enumerate(three_parts(block[...])):
            every[pl.ds(pl.multiple_of(32 * part + 8 * place, 8), 8)] = rows
    every[96:128] = jnp.zeros((32, 2 * LANES), F32)
    columns = every[...].T[0 : ORB * ORB].astype(BF16)
    for tile in range(TILES):
        pair_coef[tile] = jnp.dot(columns, chosen[:, LANES * tile : LANES * (tile + 1)], preferred_element_type=F32)
    for tile in range(TILES):
        right(tile, pair_coef, z, y)
        turn_out(tile, result, y)


def last_kernel(outer, sums, pair_coef, atom_coef, weights, done, out, natural, result, x, z, y, sem):
    core = lax.axis_index("energy") % 2
    finished = [pltpu.make_async_copy(done.at[pl.ds(ROW * half, ROW)], out.at[energy_of(2 + half, core)], sem.at[TILES + 1 + half]) for half in range(2)]
    for copy in finished:
        copy.start()
    near, far = weights[0], weights[1]
    near_part, far_part = near[:, 0:32], far[:, 0:32]

    def prepare(tile):
        for row, j in blocks_of(tile):
            rows = slice(ROW * row + 8 * j, ROW * row + 8 * j + 8)
            first = far if row else near
            for half in range(2):
                lanes = slice(128 * half, 128 * half + 128)
                total = sums[row, j, :, lanes] + first * outer[2 * NBR * half + j]
                if row == 0:
                    total = total + far * outer[2 * NBR * half + NBR + j]
                natural[rows, lanes] = total
            part, place = divmod(j, TAIL)
            total = sums[row, j, :, 256:288] + (far_part if row else near_part) * outer[4 * NBR + place, :, 32 * part : 32 * part + 32]
            if row == 0:
                total = total + far_part * outer[4 * NBR + place, :, 64 + 32 * part : 96 + 32 * part]
            natural[rows, 256:288] = total
        turn_in(tile, natural, x)

    copies, after = sender(result, out, 0, core, sem)
    prepare(0)
    for tile in range(TILES):
        if tile + 1 < TILES:
            prepare(tile + 1)
        left(tile, atom_coef, x, z)
        right(tile, pair_coef, z, y)
        turn_out(tile, result, y)
        after(tile)
    for copy in finished + copies:
        copy.wait()


def held(value):
    return pltpu.with_memory_space_constraint(value, pltpu.VMEM)


def planned(green_blocks, coupling, neighbours, freq_offset, emit_weight, absorb_weight):
    energies, atoms = lax.axis_size("energy"), lax.axis_size("atom")
    shape = lambda dims, dtype=F32: pltpu.VMEM(dims, dtype)
    vmem = pl.BlockSpec(memory_space=pltpu.VMEM)
    anywhere = pl.BlockSpec(memory_space=pl.ANY)
    green = jnp.transpose(green_blocks, (0, 2, 1, 3))
    outer, fore, rear, mine = pl.pallas_call(
        pack_kernel,
        out_shape=(shape((PACK, 8, LANES)), shape((2, NBR, ATOM, WIDTH)), shape((2, NBR, ATOM, WIDTH)), shape((ATOM, 2 * LANES))),
        in_specs=[anywhere] * 2,
        out_specs=(vmem,) * 4,
        scratch_shapes=[pltpu.VMEM((ORB, ATOM, ORB), F32), pltpu.SemaphoreType.DMA((ROWS + 1,))],
        compiler_params=pltpu.CompilerParams(vmem_limit_bytes=GRANT),
        name="pack",
    )(*(pltpu.with_memory_space_constraint(array, pltpu.HBM) for array in (green, jnp.transpose(coupling, (1, 0, 2)))))

    ends = {0: 1, energies - 1: energies - 2}
    others = {other: end for end, other in ends.items()}
    up, down = [], []
    for e in range(energies):
        for a in range(atoms):
            here, above, below = e * atoms + a, (a + 1) % atoms, (a - 1) % atoms
            if e in ends and a % 2:
                up.append((here, ends[e] * atoms + below))
                down.append((here, e * atoms + below))
            elif e in ends:
                up.append((here, e * atoms + above))
                down.append((here, ends[e] * atoms + above))
            elif e in others and a % 2:
                up.append((here, others[e] * atoms + above))
                down.append((here, e * atoms + above))
            elif e in others:
                up.append((here, e * atoms + below))
                down.append((here, others[e] * atoms + below))
            else:
                up.append((here, e * atoms + above))
                down.append((here, e * atoms + below))
    third = lax.ppermute(mine, ("energy", "atom"), up)
    first = lax.ppermute(mine, ("energy", "atom"), down)
    pairs = []
    for e in range(energies):
        for a in range(atoms):
            if e in (0, energies - 1):
                to = e * atoms + atoms - 1 - a
            else:
                to = (e + 1 if e % 2 else e - 1) * atoms + a
            pairs.append((e * atoms + a, to))
    far = lax.ppermute(outer, ("energy", "atom"), pairs)
    near = lax.ppermute(rear, "energy", [(e, e ^ 1) for e in range(energies)])
    second = lax.ppermute(mine, "atom", [(a, (a + 2) % atoms) for a in range(atoms)])
    turned = pltpu.VMEM((TILES, WIDTH, LANES), F32)
    halfway = shape((TILES, 2 * WIDTH, LANES))
    rowwise = pltpu.VMEM((TILES * LANES, WIDTH), F32)
    table = pltpu.VMEM((LANES, 2 * LANES), F32)
    rows = jax.ShapeDtypeStruct((ROWS, ROW, WIDTH), F32)
    sums, weights, chosen, atom_coef, z = pl.pallas_call(
        left_kernel,
        out_shape=(shape((2, NBR, ATOM, WIDTH)), shape((2, 8, LANES)), shape((LANES, (TILES + 1) * LANES), BF16), shape((ORB * ORB, LANES)), halfway),
        in_specs=[vmem] * 8,
        out_specs=(vmem,) * 5,
        scratch_shapes=[pltpu.VMEM((ATOM, LANES), F32), table, rowwise, turned],
        compiler_params=pltpu.CompilerParams(vmem_limit_bytes=GRANT),
        name="left",
    )(*map(held, (fore, rear, near)), neighbours, freq_offset[None], emit_weight[None], absorb_weight[None], held(mine))
    done, pair_coef = pl.pallas_call(
        right_kernel,
        out_shape=(shape((2 * ROW, WIDTH)), shape((TILES, ORB * ORB, LANES))),
        in_specs=[vmem] * 6,
        out_specs=(vmem, vmem),
        scratch_shapes=[table, turned],
        compiler_params=pltpu.CompilerParams(vmem_limit_bytes=GRANT),
        name="right",
    )(*map(held, (z, chosen, mine, first, second, third)))
    out = pl.pallas_call(
        last_kernel,
        out_shape=rows,
        in_specs=[vmem] * 6,
        out_specs=anywhere,
        scratch_shapes=[rowwise, rowwise, turned, halfway, turned, pltpu.SemaphoreType.DMA((TILES + 3,))],
        compiler_params=pltpu.CompilerParams(vmem_limit_bytes=GRANT),
        name="last",
    )(*map(held, (far, sums, pair_coef, atom_coef, weights, done)))
    return jnp.transpose(out.reshape(ROWS, NBR, ATOM, WIDTH), (0, 2, 1, 3))


def solution(mesh):
    placed = (
        P("energy", "atom", None, None),
        P("atom", None, None),
        P("atom", None),
        P(),
        P(),
        P(),
    )
    return jax.shard_map(
        planned,
        mesh=mesh,
        in_specs=placed,
        out_specs=P("energy", "atom", None, None),
        check_vma=False,
    )
```

```python
import jax
import jax.numpy as jnp
from jax import lax
from jax.experimental import pallas as pl
from jax.experimental.pallas import tpu as pltpu
from jax.sharding import PartitionSpec as P

OFF = 2
ROWS = 4
ORB = 12
NBR = 34
ATOM = 8
ROW = NBR * ATOM
WIDTH = 288
LANES = 128
TILES = 5
TAIL = 17
PACK = 4 * NBR + TAIL
F32 = jnp.float32
BF16 = jnp.bfloat16
GRANT = 16 << 20


def energy_of(row, core):
    return jnp.where(core == 0, row, ROWS - 1 - row)


def pack_kernel(green, coupling, outer, fore, rear, flat, matrices, sem):
    core = lax.axis_index("energy") % 2
    copies = []
    for row in range(ROWS):
        target = fore.at[row] if row < 2 else rear.at[row - 2]
        copies.append(pltpu.make_async_copy(green.at[energy_of(row, core)], target, sem.at[row]))
    copies.append(pltpu.make_async_copy(coupling, matrices, sem.at[ROWS]))
    for place in (0, 1, 4, 2, 3):
        copies[place].start()
    for row in range(2):
        copies[row].wait()
        outer[NBR * row : NBR * (row + 1)] = fore[row, :, :, 0:128]
        outer[NBR * (2 + row) : NBR * (3 + row)] = fore[row, :, :, 128:256]
    tails = [fore[part // 2, TAIL * (part % 2) : TAIL * (part % 2 + 1), :, 256:288] for part in range(4)]
    outer[4 * NBR : PACK] = jnp.concatenate(tails, axis=-1)
    copies[4].wait()
    pieces = [matrices[orbital] for orbital in range(ORB)] + [jnp.zeros((ATOM, 2 * LANES - ORB * ORB), F32)]
    flat[...] = jnp.concatenate(pieces, axis=-1)
    copies[2].wait()
    copies[3].wait()


def filled(tile):
    return min(LANES, 2 * ROW - LANES * tile)


FOLD = TILES - 1
SMALL = 2 * ROW - LANES * FOLD


def turn_in(tile, natural, x):
    size = filled(tile)
    rows = slice(LANES * tile, LANES * tile + size)
    if tile == FOLD:
        middle = natural[rows, 128:256].T
        x[tile, 0:128, 0:size] = natural[rows, 0:128].T
        x[tile, 128:144, 0:size] = middle[0:16]
        x[tile, 0:112, size : 2 * size] = middle[16:128]
        x[tile, 112:144, size : 2 * size] = natural[rows, 256:288].T
        return
    x[tile, 0:128, 0:size] = natural[rows, 0:128].T
    x[tile, 128:256, 0:size] = natural[rows, 128:256].T
    x[tile, 256:288, 0:size] = natural[rows, 256:288].T


def turn_out(tile, result, y):
    size = filled(tile)
    rows = slice(LANES * tile, LANES * tile + size)
    if tile == FOLD:
        result[rows, 0:128] = y[tile, 0:128, 0:size].T
        result[rows, 128:256] = jnp.concatenate([y[tile, 128:144, 0:size], y[tile, 0:112, size : 2 * size]], axis=0).T
        result[rows, 256:288] = y[tile, 112:144, size : 2 * size].T
        return
    result[rows, 0:128] = y[tile, 0:128, 0:size].T
    result[rows, 128:256] = y[tile, 128:256, 0:size].T
    result[rows, 256:288] = y[tile, 256:288, 0:size].T


def blocks_of(tile):
    return [divmod(block, NBR) for block in range(16 * tile, 16 * tile + filled(tile) // 8)]


def left(tile, atom_coef, x, z):
    low = lax.broadcasted_iota(jnp.int32, (8, LANES), 0) < 4
    parts = range(1 if tile == FOLD else 2)
    for block in range(0, ORB, 6):
        totals = {}
        for pair in range(6):
            values = [[x[tile, pl.ds(144 * part + 24 * pair + 8 * k, 8)] for k in range(3)] for part in parts]
            for a in range(block, block + 6):
                first = jnp.broadcast_to(atom_coef[ORB * a + 2 * pair : ORB * a + 2 * pair + 1], (8, LANES))
                last = jnp.broadcast_to(atom_coef[ORB * a + 2 * pair + 1 : ORB * a + 2 * pair + 2], (8, LANES))
                coef = (first, jnp.where(low, first, last), last)
                for part in parts:
                    for k in range(3):
                        term = coef[k] * values[part][k]
                        totals[a, part, k] = term if pair == 0 else totals[a, part, k] + term
        for (a, part, k), total in totals.items():
            z[tile, pl.ds((ORB * part + a) * 24 + 8 * k, 8)] = total


def right(tile, pair_coef, z, y):
    totals = {}
    groups = range(2 if tile == FOLD else 3)
    for d in range(ORB):
        values = [z[tile, pl.ds(192 * k + d, 8, stride=24)] + z[tile, pl.ds(192 * k + 12 + d, 8, stride=24)] for k in groups]
        for f in range(ORB):
            coef = jnp.broadcast_to(pair_coef[tile, ORB * f + d : ORB * f + d + 1], (8, LANES))
            for k in groups:
                term = coef * values[k]
                totals[f, k] = term if d == 0 else totals[f, k] + term
    for (f, k), total in totals.items():
        y[tile, pl.ds(96 * k + f, 8, stride=ORB)] = total


def three_parts(rows):
    high = rows.astype(BF16).astype(F32)
    mid = (rows - high).astype(BF16).astype(F32)
    return high, mid, rows - high - mid


def kernel_values(freq, emit, absorb, sign):
    sums = []
    for d in range(-OFF, OFF + 1):
        shift = d * sign
        terms = jnp.where(freq == -shift, emit, 0.0) + jnp.where(freq == shift, absorb, 0.0)
        sums.append(jnp.sum(terms, axis=1, keepdims=True))
    return sums


def left_kernel(fore, rear, near, neighbours, freq, emit, absorb, mine, sums, weights, chosen, atom_coef, z,
                indices, every, natural, x):
    position = lax.axis_index("energy")
    core = position % 2
    weight = kernel_values(freq[...], emit[...], absorb[...], 1 - 2 * core)
    inside = jnp.where((position > 0) & (position < lax.axis_size("energy") - 1), 1.0, 0.0).astype(F32)
    for place, value in enumerate((weight[1] * inside, weight[0] * inside)):
        weights[place] = jnp.broadcast_to(value, (8, LANES))
    indices[...] = jnp.zeros_like(indices)
    indices[:, 0:NBR] = neighbours[...].astype(F32)
    width = TILES * LANES
    lane = lax.broadcasted_iota(jnp.int32, (LANES, width), 1)
    lane = lane - jnp.where(lane >= 2 * ROW, SMALL, 0)
    within = lane - jnp.where(lane >= ROW, ROW, 0)
    picks = (lax.shift_right_logical(within, 3) == lax.broadcasted_iota(jnp.int32, (LANES, width), 0)).astype(F32).astype(BF16)
    spread = jnp.dot(indices[...].astype(BF16), picks, preferred_element_type=F32)
    lane8 = lax.broadcasted_iota(jnp.int32, (ATOM, width), 1) & 7
    own = lane8 == lax.broadcasted_iota(jnp.int32, (ATOM, width), 0)
    listed = jnp.sum(jnp.where(own, spread, 0.0), axis=0, keepdims=True)
    listed = listed - (lax.axis_index("atom") * ATOM).astype(F32)
    listed = jnp.where(listed < 0, listed + 32.0, listed)
    number = (lax.broadcasted_iota(jnp.int32, (LANES, width), 0) & 31).astype(F32)
    chosen[:, 0:width] = (number == listed).astype(F32).astype(BF16)
    spots = (lax.broadcasted_iota(jnp.int32, (LANES, LANES), 0) & 31) == (lax.broadcasted_iota(jnp.int32, (LANES, LANES), 1) & 7)
    chosen[:, width : width + LANES] = spots.astype(F32).astype(BF16)

    every[...] = jnp.zeros_like(every)
    for place, part in enumerate(three_parts(mine[...])):
        every[32 * place : 32 * place + 8] = part
    columns = every[...].T[0 : ORB * ORB].astype(BF16)
    atom_coef[...] = jnp.dot(columns, chosen[:, width : width + LANES], preferred_element_type=F32)
    sources = [(fore, 0), (fore, 1), (rear, 0), (rear, 1), (near, 1), (near, 0)]

    def energy_sum(row, j):
        total = None
        for source in range(max(0, row - OFF), min(ROWS + OFF, row + OFF + 1)):
            ref, place = sources[source]
            term = weight[source - row + OFF] * ref[place, j]
            total = term if total is None else total + term
        return total

    def prepare(tile):
        for row, j in blocks_of(tile):
            natural[ROW * row + 8 * j : ROW * row + 8 * j + 8] = energy_sum(2 + row, j)
            sums[row, j] = energy_sum(row, j)
        turn_in(tile, natural, x)

    prepare(0)
    for tile in range(TILES):
        if tile + 1 < TILES:
            prepare(tile + 1)
        left(tile, atom_coef, x, z)


def sender(result, out, first_row, core, sem):
    pieces = []
    for tile in range(TILES):
        for half in range(2):
            low, high = max(LANES * tile, ROW * half), min(LANES * (tile + 1), ROW * (half + 1))
            if low < high:
                target = out.at[energy_of(first_row + half, core), pl.ds(low - ROW * half, high - low)]
                pieces.append((tile, pltpu.make_async_copy(result.at[pl.ds(low, high - low)], target, sem.at[len(pieces)])))

    def after(tile):
        for ready, piece in pieces:
            if ready == tile:
                piece.start()

    return [piece for _, piece in pieces], after


def right_kernel(z, chosen, mine, from_next, from_second, from_third, result, pair_coef, every, y):
    position = lax.axis_index("energy")
    crossed = jnp.where((position == 1) | (position == lax.axis_size("energy") - 2), 1, 0)
    for place, block in ((0, mine), (1 + 2 * crossed, from_next), (2, from_second), (3 - 2 * crossed, from_third)):
        for part, rows in enumerate(three_parts(block[...])):
            every[pl.ds(pl.multiple_of(32 * part + 8 * place, 8), 8)] = rows
    every[96:128] = jnp.zeros((32, 2 * LANES), F32)
    columns = every[...].T[0 : ORB * ORB].astype(BF16)
    for tile in range(TILES):
        pair_coef[tile] = jnp.dot(columns, chosen[:, LANES * tile : LANES * (tile + 1)], preferred_element_type=F32)
    for tile in range(TILES):
        right(tile, pair_coef, z, y)
        turn_out(tile, result, y)


def last_kernel(outer, sums, pair_coef, atom_coef, weights, done, out, natural, result, x, z, y, sem):
    core = lax.axis_index("energy") % 2
    finished = [pltpu.make_async_copy(done.at[pl.ds(ROW * half, ROW)], out.at[energy_of(2 + half, core)], sem.at[TILES + 1 + half]) for half in range(2)]
    near, far = weights[0], weights[1]
    near_part, far_part = near[:, 0:32], far[:, 0:32]

    def prepare(tile):
        for row, j in blocks_of(tile):
            rows = slice(ROW * row + 8 * j, ROW * row + 8 * j + 8)
            first = far if row else near
            for half in range(2):
                lanes = slice(128 * half, 128 * half + 128)
                total = sums[row, j, :, lanes] + first * outer[2 * NBR * half + j]
                if row == 0:
                    total = total + far * outer[2 * NBR * half + NBR + j]
                natural[rows, lanes] = total
            part, place = divmod(j, TAIL)
            total = sums[row, j, :, 256:288] + (far_part if row else near_part) * outer[4 * NBR + place, :, 32 * part : 32 * part + 32]
            if row == 0:
                total = total + far_part * outer[4 * NBR + place, :, 64 + 32 * part : 96 + 32 * part]
            natural[rows, 256:288] = total
        turn_in(tile, natural, x)

    copies, after = sender(result, out, 0, core, sem)
    prepare(0)
    for copy in finished:
        copy.start()
    prepare(1)
    for tile in range(TILES):
        left(tile, atom_coef, x, z)
        if tile > 0:
            turn_out(tile - 1, result, y)
            after(tile - 1)
        if tile + 2 < TILES:
            prepare(tile + 2)
        right(tile, pair_coef, z, y)
    turn_out(TILES - 1, result, y)
    after(TILES - 1)
    for copy in finished + copies:
        copy.wait()


def held(value):
    return pltpu.with_memory_space_constraint(value, pltpu.VMEM)


def planned(green_blocks, coupling, neighbours, freq_offset, emit_weight, absorb_weight):
    energies, atoms = lax.axis_size("energy"), lax.axis_size("atom")
    shape = lambda dims, dtype=F32: pltpu.VMEM(dims, dtype)
    vmem = pl.BlockSpec(memory_space=pltpu.VMEM)
    anywhere = pl.BlockSpec(memory_space=pl.ANY)
    green = jnp.transpose(green_blocks, (0, 2, 1, 3))
    outer, fore, rear, mine = pl.pallas_call(
        pack_kernel,
        out_shape=(shape((PACK, 8, LANES)), shape((2, NBR, ATOM, WIDTH)), shape((2, NBR, ATOM, WIDTH)), shape((ATOM, 2 * LANES))),
        in_specs=[anywhere] * 2,
        out_specs=(vmem,) * 4,
        scratch_shapes=[pltpu.VMEM((ORB, ATOM, ORB), F32), pltpu.SemaphoreType.DMA((ROWS + 1,))],
        compiler_params=pltpu.CompilerParams(vmem_limit_bytes=GRANT),
        name="pack",
    )(*(pltpu.with_memory_space_constraint(array, pltpu.HBM) for array in (green, jnp.transpose(coupling, (1, 0, 2)))))

    ends = {0: 1, energies - 1: energies - 2}
    others = {other: end for end, other in ends.items()}
    up, down = [], []
    for e in range(energies):
        for a in range(atoms):
            here, above, below = e * atoms + a, (a + 1) % atoms, (a - 1) % atoms
            if e in ends and a % 2:
                up.append((here, ends[e] * atoms + below))
                down.append((here, e * atoms + below))
            elif e in ends:
                up.append((here, e * atoms + above))
                down.append((here, ends[e] * atoms + above))
            elif e in others and a % 2:
                up.append((here, others[e] * atoms + above))
                down.append((here, e * atoms + above))
            elif e in others:
                up.append((here, e * atoms + below))
                down.append((here, others[e] * atoms + below))
            else:
                up.append((here, e * atoms + above))
                down.append((here, e * atoms + below))
    third = lax.ppermute(mine, ("energy", "atom"), up)
    first = lax.ppermute(mine, ("energy", "atom"), down)
    pairs = []
    for e in range(energies):
        for a in range(atoms):
            if e in (0, energies - 1):
                to = e * atoms + atoms - 1 - a
            else:
                to = (e + 1 if e % 2 else e - 1) * atoms + a
            pairs.append((e * atoms + a, to))
    far = lax.ppermute(outer, ("energy", "atom"), pairs)
    near = lax.ppermute(rear, "energy", [(e, e ^ 1) for e in range(energies)])
    second = lax.ppermute(mine, "atom", [(a, (a + 2) % atoms) for a in range(atoms)])
    turned = pltpu.VMEM((TILES, WIDTH, LANES), F32)
    halfway = shape((TILES, 2 * WIDTH, LANES))
    rowwise = pltpu.VMEM((TILES * LANES, WIDTH), F32)
    table = pltpu.VMEM((LANES, 2 * LANES), F32)
    rows = jax.ShapeDtypeStruct((ROWS, ROW, WIDTH), F32)
    sums, weights, chosen, atom_coef, z = pl.pallas_call(
        left_kernel,
        out_shape=(shape((2, NBR, ATOM, WIDTH)), shape((2, 8, LANES)), shape((LANES, (TILES + 1) * LANES), BF16), shape((ORB * ORB, LANES)), halfway),
        in_specs=[vmem] * 8,
        out_specs=(vmem,) * 5,
        scratch_shapes=[pltpu.VMEM((ATOM, LANES), F32), table, rowwise, turned],
        compiler_params=pltpu.CompilerParams(vmem_limit_bytes=GRANT),
        name="left",
    )(*map(held, (fore, rear, near)), neighbours, freq_offset[None], emit_weight[None], absorb_weight[None], held(mine))
    done, pair_coef = pl.pallas_call(
        right_kernel,
        out_shape=(shape((2 * ROW, WIDTH)), shape((TILES, ORB * ORB, LANES))),
        in_specs=[vmem] * 6,
        out_specs=(vmem, vmem),
        scratch_shapes=[table, turned],
        compiler_params=pltpu.CompilerParams(vmem_limit_bytes=GRANT),
        name="right",
    )(*map(held, (z, chosen, mine, first, second, third)))
    out = pl.pallas_call(
        last_kernel,
        out_shape=rows,
        in_specs=[vmem] * 6,
        out_specs=anywhere,
        scratch_shapes=[rowwise, rowwise, turned, halfway, turned, pltpu.SemaphoreType.DMA((TILES + 3,))],
        compiler_params=pltpu.CompilerParams(vmem_limit_bytes=GRANT),
        name="last",
    )(*map(held, (far, sums, pair_coef, atom_coef, weights, done)))
    return jnp.transpose(out.reshape(ROWS, NBR, ATOM, WIDTH), (0, 2, 1, 3))


def solution(mesh):
    placed = (
        P("energy", "atom", None, None),
        P("atom", None, None),
        P("atom", None),
        P(),
        P(),
        P(),
    )
    return jax.shard_map(
        planned,
        mesh=mesh,
        in_specs=placed,
        out_specs=P("energy", "atom", None, None),
        check_vma=False,
    )
```
